32 devices in a mesh: groups: 1, row: 16 (over z, y, x), col: 2 (over core).
Axes of the slice: x: 2, y: 2, z: 4, core: 2. Of those that a mesh axis runs over, the one named last changes fastest.
Arguments:
- image: bfloat16 [64, 64, 1408], P(('groups', 'row'), None, 'col'), may hold values from -6 to 6
- kernel: float32 [7, 7, 1408], P(None, None, 'col'), may hold values from -0.875 to 0.875
- ln_gain: float32 [1408], replicated, may hold values from 0.1 to 1.9
- ln_bias: float32 [1408], replicated, may hold values from -3 to 3
- layer_scale: float32 [1408], replicated, may hold values from 0.3 to 1.5
- w_in: bfloat16 [1408, 2816], P('row', 'col'), may hold values from -0.15625 to 0.15625
- w_out: bfloat16 [2816, 1408], P('col', 'row'), may hold values from -0.109375 to 0.109375
- cotangent: bfloat16 [64, 64, 1408], P(('groups', 'row'), None, 'col'), may hold values from -16 to 16
Outputs:
- result: bfloat16 [64, 64, 1408], P(('groups', 'row'), None, 'col')
- grad_image: bfloat16 [64, 64, 1408], P(('groups', 'row'), None, 'col')
- grad_kernel: float32 [7, 7, 1408], P('groups', None, 'col')
- grad_params: float32 [3, 1408], P('groups', 'col')
The draws below stay inside these ranges and needn't reach their ends.
All inputs are finite; a program needn't handle non-finite values.
Results may differ from the reference program's by a relative error of at most 0.0057.
Values may be sent and summed in bfloat16 or wider, within the bound.
No kernel may reach another device: no remote copies, remote signals or barrier semaphores. Data moves between devices by JAX's collectives and lax.ppermute only.
A program may use at most 64 MiB of HBM per device.

```python
import math
import jax
import jax.numpy as jnp
from jax import lax

C = 1408
F = 2816
SLAB_ROWS = 4
GRID_COLS = 64
ROWS = 64


def draw_cotangent(key, part):
    position = jnp.arange(ROWS, dtype=jnp.float32)[:, None, None] / (ROWS - 1)
    base = jnp.clip(jax.random.normal(key, (ROWS, GRID_COLS, C), jnp.float32), -4.0, 4.0)
    factor = 1.0 + 2.0 * position
    return (base * factor).astype(jnp.bfloat16)


def steps_of(stream_key, extent, shards, least, high):
    loudness = 1.0
    for dim, blocks in shards:
        steps = jax.random.uniform(jax.random.fold_in(jax.random.fold_in(stream_key, 6), dim), (blocks,), jnp.float32, least / len(shards), high / len(shards))
        loudness = loudness * jnp.repeat(jnp.exp(steps), extent[dim] // blocks).reshape((-1,) + (1,) * (len(extent) - 1 - dim))
    return loudness


def bell_draw(own_key, shape, scale, most, pieces=(), kind=jnp.bfloat16):
    values = jax.random.normal(own_key, shape, jnp.float32) * scale
    if len(pieces) > 0:
        values = steps_of(own_key, shape, pieces, -0.22, 0.18) * values
    return jnp.clip(values, min=-most, max=most).astype(kind)


def setup_inputs(seed: int = 0, part: int = 0) -> dict:
    streams_of = jax.random.split(jax.random.key(seed), 9)
    own_keys = jax.random.split(jax.random.fold_in(streams_of[8], part), 9)
    image = bell_draw(own_keys[0], (ROWS, GRID_COLS, C), 1.0, 6.0, ((0, 16), (2, 2)))
    kernel = bell_draw(streams_of[1], (7, 7, C), 49 ** -0.5, 0.875, ((2, 2),), jnp.float32)
    ln_gain = jnp.clip(1.0 + 0.18 * jax.random.normal(streams_of[2], (C,), jnp.float32), 0.1, 1.9)
    ln_bias = bell_draw(streams_of[3], (C,), 0.5, 3.0, (), jnp.float32)
    layer_scale = jnp.clip(jnp.exp(jax.random.uniform(streams_of[4], (C,), jnp.float32, math.log(0.3), math.log(1.5))), 0.3, 1.5)
    w_in = bell_draw(streams_of[5], (C, F), C ** -0.5, 0.15625, ((0, 16), (1, 2)))
    w_out = bell_draw(streams_of[6], (F, C), F ** -0.5, 0.109375, ((0, 2), (1, 16)))
    cotangent = draw_cotangent(jax.random.fold_in(jax.random.fold_in(streams_of[8], part), 71), part)
    return {"image": image, "kernel": kernel, "ln_gain": ln_gain, "ln_bias": ln_bias, "layer_scale": layer_scale, "w_in": w_in, "w_out": w_out, "cotangent": cotangent}


epsilon = 1e-06

def depthwise(padded, kernel, height, breadth):
    output = jnp.zeros((height, breadth, kernel.shape[2]), jnp.float32)
    for row_tap in range(7):
        for col_tap in range(7):
            output = output + kernel[row_tap, col_tap] * padded[row_tap:row_tap + height, col_tap:col_tap + breadth]
    return output

def transposed(padded, kernel, height, breadth):
    output = jnp.zeros((height, breadth, kernel.shape[2]), jnp.float32)
    for row_tap in range(7):
        for col_tap in range(7):
            output = output + kernel[row_tap, col_tap] * padded[6 - row_tap:6 - row_tap + height, 6 - col_tap:6 - col_tap + breadth]
    return output

def kernel_grad(grad_field, padded, height, breadth):
    return jnp.stack([jnp.stack([lax.optimization_barrier(jnp.sum(grad_field * padded[row_tap:row_tap + height, col_tap:col_tap + breadth], axis=(0, 1))) for col_tap in range(7)]) for row_tap in range(7)])

def gelu_slope(values):
    cumulative = 0.5 * (1.0 + lax.erf(values * (1.0 / math.sqrt(2.0))))
    return cumulative + values * jnp.exp(-0.5 * values * values) * (1.0 / math.sqrt(2.0 * math.pi))

def reference(image, kernel, ln_gain, ln_bias, layer_scale, w_in, w_out, cotangent):
    height, breadth, channels = image.shape
    source = image.astype(jnp.float32)
    padded = jnp.pad(source, ((3, 3), (3, 3), (0, 0)))
    conved = depthwise(padded, kernel, height, breadth)
    average = lax.optimization_barrier(jnp.mean(conved, axis=2, keepdims=True))
    centred = conved - average
    inv_std = lax.rsqrt(lax.optimization_barrier(jnp.mean(centred * centred, axis=2, keepdims=True)) + epsilon)
    normal_part = centred * inv_std
    normed = (normal_part * ln_gain + ln_bias).astype(jnp.bfloat16)
    cot_float = cotangent.astype(jnp.float32)
    scaled = (cot_float * layer_scale).astype(jnp.bfloat16)
    blocks = height * breadth // (SLAB_ROWS * GRID_COLS)

    def mlp(pair):
        normed_rows, scaled_rows = pair
        hidden = jnp.dot(normed_rows, w_in, preferred_element_type=jnp.float32)
        activated = jax.nn.gelu(hidden, approximate=False).astype(jnp.bfloat16)
        branch_rows = jnp.dot(activated, w_out, preferred_element_type=jnp.float32)
        act_grad = jnp.dot(scaled_rows, w_out.T, preferred_element_type=jnp.float32)
        hid_grad = (act_grad * gelu_slope(hidden)).astype(jnp.bfloat16)
        return (branch_rows, jnp.dot(hid_grad, w_in.T, preferred_element_type=jnp.float32))
    branch, norm_grad = lax.map(mlp, (normed.reshape(blocks, -1, channels), scaled.reshape(blocks, -1, channels)))
    branch = branch.reshape(height, breadth, channels)
    norm_grad = norm_grad.reshape(height, breadth, channels)
    result = (source + layer_scale * branch).astype(jnp.bfloat16)
    grad_hat = norm_grad * ln_gain
    conv_grad = inv_std * (grad_hat - lax.optimization_barrier(jnp.mean(grad_hat, axis=2, keepdims=True)) - normal_part * lax.optimization_barrier(jnp.mean(grad_hat * normal_part, axis=2, keepdims=True)))
    grad_padded = jnp.pad(conv_grad, ((3, 3), (3, 3), (0, 0)))
    grad_image = (cot_float + transposed(grad_padded, kernel, height, breadth)).astype(jnp.bfloat16)
    factor = 1.0 / math.sqrt(height * breadth)
    grad_kernel = kernel_grad(conv_grad, padded, height, breadth) * factor
    grad_params = jnp.stack([lax.optimization_barrier(jnp.sum(norm_grad * normal_part, axis=(0, 1))), lax.optimization_barrier(jnp.sum(norm_grad, axis=(0, 1))), lax.optimization_barrier(jnp.sum(cot_float * branch, axis=(0, 1)))]) * factor
    return (result, grad_image, grad_kernel, grad_params)
```

```python
import math

import jax
import jax.numpy as jnp
from jax import lax
from jax.experimental import pallas as pl
from jax.experimental.pallas import tpu as pltpu
from jax.sharding import PartitionSpec as P

epsilon = 1e-06


def exchanged(value, mask):
    count = lax.axis_size("row")
    return lax.ppermute(value, "row", [(i, i ^ mask) for i in range(count)])


def siblings(value):
    return lax.ppermute(value, "col", [(0, 1), (1, 0)])


def edges(block, width):
    count = lax.axis_size("row")
    forward = [(i, i + 1) for i in range(count - 1)]
    backward = [(i + 1, i) for i in range(count - 1)]
    low = lax.ppermute(block[block.shape[0] - width :], "row", forward)
    high = lax.ppermute(block[:width], "row", backward)
    return low, high


def gathered(shard, first, second):
    count = lax.axis_size("row")
    rows, width = shard.shape
    if count != 16:
        return lax.all_gather(shard, "row", axis=0, tiled=True)
    blocks = {0: shard}
    blocks[4] = exchanged(shard, 4)
    blocks[8] = exchanged(shard, 8)
    blocks[12] = exchanged(blocks[8], 4)
    for far in (0, 4, 8, 12):
        blocks[far + first] = exchanged(blocks[far], first)
        blocks[far + second] = exchanged(blocks[far], second)
        blocks[far + 3] = exchanged(blocks[far + first], second)
    place = lax.axis_index("row")
    whole = jnp.zeros((count * rows, width), shard.dtype)
    for mask, block in blocks.items():
        whole = lax.dynamic_update_slice(whole, block, ((place ^ mask) * rows, 0))
    return whole


def summed(value):
    count = lax.axis_size("row")
    if count & (count - 1):
        return lax.psum(value, "row")
    mask = 1
    while mask < count:
        value = value + exchanged(value, mask)
        mask *= 2
    return value


def depthwise(padded, kernel, height, breadth, flip):
    output = jnp.zeros((height, breadth, kernel.shape[2]), jnp.float32)
    for row_tap in range(7):
        for col_tap in range(7):
            row, col = (6 - row_tap, 6 - col_tap) if flip else (row_tap, col_tap)
            output = (
                output
                + kernel[row_tap, col_tap] * padded[row : row + height, col : col + breadth]
            )
    return output


def spans(extent, step):
    return [(at, min(step, extent - at)) for at in range(0, extent, step)]


def mlp_body(
    column, normed, scaled, w_in, w_out, branch_own, branch_far, norm_own, norm_far, act, grad
):
    width = w_in.shape[1]
    part = branch_own.shape[1]
    for at, size in spans(width, 256):
        lanes = slice(at, at + size)
        hidden = jnp.dot(normed[...], w_in[:, lanes], preferred_element_type=jnp.float32)
        act_grad = jnp.dot(scaled[...], w_out[:, lanes], preferred_element_type=jnp.float32)
        cumulative = 0.5 * (1.0 + lax.erf(hidden * (1.0 / math.sqrt(2.0))))
        slope = cumulative + hidden * jnp.exp(-0.5 * hidden * hidden) * (
            1.0 / math.sqrt(2.0 * math.pi)
        )
        act[:, lanes] = (hidden * cumulative).astype(jnp.bfloat16)
        grad[:, lanes] = (act_grad * slope).astype(jnp.bfloat16)
    own = pl.multiple_of(column[0] * part, part)
    far = pl.multiple_of((1 - column[0]) * part, part)
    contract = (((1,), (1,)), ((), ()))
    for left, weights, outs in (
        (grad, w_in, ((norm_far, far), (norm_own, own))),
        (act, w_out, ((branch_far, far), (branch_own, own))),
    ):
        for out, start in outs:
            for at, size in spans(part, 256):
                out[:, at : at + size] = lax.dot_general(
                    left[...],
                    weights[pl.ds(start + at, size), :],
                    contract,
                    preferred_element_type=jnp.float32,
                )


def mlp(column, normed, scaled, w_in, w_out):
    tokens, channels = normed.shape
    width = w_in.shape[1]
    part = jax.ShapeDtypeStruct((tokens, channels // 2), jnp.float32)
    return pl.pallas_call(
        mlp_body,
        out_shape=(part,) * 4,
        in_specs=[pl.BlockSpec(memory_space=pltpu.SMEM)]
        + [pl.BlockSpec(memory_space=pltpu.VMEM)] * 4,
        out_specs=(pl.BlockSpec(memory_space=pltpu.VMEM),) * 4,
        scratch_shapes=[pltpu.VMEM((tokens, width), jnp.bfloat16)] * 2,
        compiler_params=pltpu.CompilerParams(vmem_limit_bytes=32 << 20),
        cost_estimate=pl.CostEstimate(
            flops=8 * tokens * channels * width,
            bytes_accessed=4 * channels * width + 16 * tokens * channels,
            transcendentals=2 * tokens * width,
        ),
        name="mlp",
    )(column.reshape(1), normed, scaled, w_in, w_out)


def local(image, kernel, ln_gain, ln_bias, layer_scale, w_in, w_out, cotangent):
    slab_rows, grid_cols, width_part = image.shape
    tokens = slab_rows * grid_cols
    channels = ln_gain.shape[0]
    column = lax.axis_index("col").astype(jnp.int32)
    gain_part = lax.dynamic_slice_in_dim(ln_gain, column * width_part, width_part)
    bias_part = lax.dynamic_slice_in_dim(ln_bias, column * width_part, width_part)
    scale_part = lax.dynamic_slice_in_dim(layer_scale, column * width_part, width_part)
    low, high = edges(image, 3)
    w_in_all = gathered(w_in, 2, 1)
    w_out_all = gathered(w_out.T, 1, 2)
    extended = jnp.concatenate([low, image, high], axis=0)
    padded = jnp.pad(extended.astype(jnp.float32), ((0, 0), (3, 3), (0, 0)))
    conved = depthwise(padded, kernel, slab_rows, grid_cols, False).reshape(tokens, width_part)
    totals, squares = lax.psum((jnp.sum(conved, axis=1), jnp.sum(conved * conved, axis=1)), "col")
    average = totals / channels
    variance = squares / channels - average * average
    inv_std = lax.rsqrt(variance + epsilon)[:, None]
    normal_part = (conved - average[:, None]) * inv_std
    normed = lax.all_gather(
        (normal_part * gain_part + bias_part).astype(jnp.bfloat16), "col", axis=1, tiled=True
    )
    cot_float = cotangent.reshape(tokens, width_part).astype(jnp.float32)
    scaled = lax.all_gather(
        (cot_float * scale_part).astype(jnp.bfloat16), "col", axis=1, tiled=True
    )
    branch_own, branch_far, norm_own, norm_far = mlp(column, normed, scaled, w_in_all, w_out_all)
    norm_grad = norm_own + siblings(norm_far)
    branch = branch_own + siblings(branch_far)
    result = (image.reshape(tokens, width_part).astype(jnp.float32) + scale_part * branch).astype(
        jnp.bfloat16
    )
    grad_hat = norm_grad * gain_part
    first_sum, second_sum = lax.psum(
        (jnp.sum(grad_hat, axis=1), jnp.sum(grad_hat * normal_part, axis=1)), "col"
    )
    conv_grad = inv_std * (
        grad_hat - first_sum[:, None] / channels - normal_part * (second_sum[:, None] / channels)
    )
    grad_field = conv_grad.reshape(slab_rows, grid_cols, width_part)
    low, high = edges(grad_field.astype(jnp.bfloat16), 3)
    grad_extended = jnp.concatenate(
        [low.astype(jnp.float32), grad_field, high.astype(jnp.float32)], axis=0
    )
    grad_padded = jnp.pad(grad_extended, ((0, 0), (3, 3), (0, 0)))
    grad_image = (
        cot_float.reshape(slab_rows, grid_cols, width_part)
        + depthwise(grad_padded, kernel, slab_rows, grid_cols, True)
    ).astype(jnp.bfloat16)
    terms = [
        jnp.sum(
            grad_field * padded[row_tap : row_tap + slab_rows, col_tap : col_tap + grid_cols],
            axis=(0, 1),
        )
        for row_tap in range(7)
        for col_tap in range(7)
    ]
    terms += [
        jnp.sum(norm_grad * normal_part, axis=0),
        jnp.sum(norm_grad, axis=0),
        jnp.sum(cot_float * branch, axis=0),
    ]
    factor = 1.0 / math.sqrt(tokens * lax.axis_size("row"))
    sums = summed(jnp.stack(terms)) * factor
    return (
        result.reshape(slab_rows, grid_cols, width_part),
        grad_image,
        sums[:49].reshape(7, 7, width_part),
        sums[49:],
    )


def solution(mesh):
    in_specs = (
        P(("groups", "row"), None, "col"),
        P(None, None, "col"),
        P(),
        P(),
        P(),
        P("row", "col"),
        P("col", "row"),
        P(("groups", "row"), None, "col"),
    )
    out_specs = (
        P(("groups", "row"), None, "col"),
        P(("groups", "row"), None, "col"),
        P("groups", None, "col"),
        P("groups", "col"),
    )
    return jax.shard_map(local, mesh=mesh, in_specs=in_specs, out_specs=out_specs, check_vma=False)
```

```python
import functools
import math

import jax
import jax.numpy as jnp
from jax import lax
from jax.experimental import pallas as pl
from jax.experimental.pallas import tpu as pltpu
from jax.sharding import PartitionSpec as P

epsilon = 1e-06
VMEM = pl.BlockSpec(memory_space=pltpu.VMEM)
SMEM = pl.BlockSpec(memory_space=pltpu.SMEM)


def sent(value, axis, pairs):
    if value.ndim == 2 and value.shape[1] == 704:
        return lax.ppermute(value.reshape(4, -1, 704), axis, pairs).reshape(value.shape)
    return lax.ppermute(value, axis, pairs)


def exchanged(value, mask):
    count = lax.axis_size("row")
    return sent(value, "row", [(i, i ^ mask) for i in range(count)])


def siblings(value):
    return sent(value, "col", [(0, 1), (1, 0)])


def both(value):
    rows, width = value.shape
    pair = lax.all_gather(value.reshape(4, rows // 4, width), "col", axis=0, tiled=False)
    return pair.reshape(2, rows, width)


def after(value, *others):
    return lax.optimization_barrier((value, *others))[0]


def edges(even, low_rows, high_rows):
    return jnp.where(even, high_rows, low_rows), jnp.where(even, low_rows, high_rows)


def neighbours(direct, handed):
    count = lax.axis_size("row")
    through = exchanged(handed, 1)
    pairs = [(i, i + 2) for i in range(0, count - 2, 2)] + [(i, i - 2) for i in range(3, count, 2)]
    return exchanged(direct, 1), lax.ppermute(through, "row", pairs)


def call(body, outs, operands, name, scalars=(), scratch=(), flops=0, limit=24):
    moved = sum(math.prod(o.shape) * o.dtype.itemsize for o in list(outs) + list(operands))
    return pl.pallas_call(
        body,
        out_shape=tuple(outs),
        in_specs=[SMEM] * len(scalars) + [VMEM] * len(operands),
        out_specs=(VMEM,) * len(outs),
        scratch_shapes=list(scratch),
        compiler_params=pltpu.CompilerParams(vmem_limit_bytes=limit << 20),
        cost_estimate=pl.CostEstimate(flops=flops, bytes_accessed=moved, transcendentals=0),
        name=name,
    )(*scalars, *operands)


def spans(extent, step):
    return [(at, min(step, extent - at)) for at in range(0, extent, step)]


def f32(*shape):
    return jax.ShapeDtypeStruct(shape, jnp.float32)


def bf16(*shape):
    return jax.ShapeDtypeStruct(shape, jnp.bfloat16)


def each_lanes(width, body):
    full = width // 128

    def step(index, carry):
        body(pl.ds(pl.multiple_of(index * 128, 128), 128))
        return carry

    lax.fori_loop(0, full, step, 0)
    if width % 128:
        body(pl.ds(full * 128, width % 128))


def fill(rows_all, place, near, middle, beyond):
    rows = middle.shape[0]
    even = jnp.bitwise_and(place[0], 1) == 0
    rows_all[3 : 3 + rows] = middle[...].astype(jnp.float32)

    @pl.when(even)
    def _():
        rows_all[0:3] = beyond[...].astype(jnp.float32)
        rows_all[3 + rows :] = near[...].astype(jnp.float32)

    @pl.when(jnp.logical_not(even))
    def _():
        rows_all[0:3] = near[...].astype(jnp.float32)
        rows_all[3 + rows :] = beyond[...].astype(jnp.float32)


def clear_borders(ref, breadth):
    edge = ref.shape[:-2] + (8, ref.shape[-1])
    ref[..., 0:8, :] = jnp.zeros(edge, jnp.float32)
    ref[..., 8 + breadth :, :] = jnp.zeros(edge, jnp.float32)


def filtered(rows_all, kernel, shifted, rows, breadth, lanes, flip):
    size = lanes.size
    for col in range(7):
        total = [None] * rows
        for row in range(rows + 6):
            block = rows_all[row, :, lanes]
            for tap in range(7):
                at = row - tap
                if 0 <= at < rows:
                    a, b = (6 - tap, 6 - col) if flip else (tap, col)
                    term = kernel[a, b : b + 1, lanes] * block
                    total[at] = term if total[at] is None else total[at] + term
        for at in range(rows):
            shifted[col, at, 8 : 8 + breadth, 0:size] = total[at]
    results = []
    for at in range(rows):
        value = shifted[0, at, 5 : 5 + breadth, 0:size]
        for col in range(1, 7):
            value = value + shifted[col, at, 5 + col : 5 + col + breadth, 0:size]
        results.append(value)
    return results


def conv_body(place, near, middle, beyond, kernel, conved, stats, rows_all, shifted):
    rows, breadth, width = middle.shape
    fill(rows_all, place, near, middle, beyond)
    clear_borders(shifted, breadth)

    def part(lanes):
        for row, value in enumerate(filtered(rows_all, kernel, shifted, rows, breadth, lanes, False)):
            conved[row * breadth : (row + 1) * breadth, lanes] = value

    each_lanes(width, part)
    values = conved[...]
    mean = jnp.sum(values, axis=1, keepdims=True) * (1.0 / width)
    centred = values - mean
    stats[:, 0:1] = mean
    stats[:, 1:2] = jnp.sum(centred * centred, axis=1, keepdims=True)


def norm_body(conved, mine, other, params, normal, inverse, normed):
    width = conved.shape[1]
    average = 0.5 * (mine[:, 0:1] + other[:, 0:1])
    apart = mine[:, 0:1] - other[:, 0:1]
    variance = (mine[:, 1:2] + other[:, 1:2]) * (0.5 / width) + 0.25 * apart * apart
    inv_std = lax.rsqrt(variance + epsilon)
    value = (conved[...] - average) * inv_std
    normal[...] = value
    inverse[...] = inv_std
    normed[...] = (value * params[0:1, :] + params[1:2, :]).astype(jnp.bfloat16)


def split_of(width):
    main = width // 2 // 128 * 128
    return main, width // 2 - main


def packed(w_in, w_out, which):
    main, tail = split_of(w_in.shape[1])
    mains = slice(which * main, (which + 1) * main)
    tails = slice(2 * main + which * tail, 2 * main + (which + 1) * tail)
    return jnp.concatenate(
        [w_in[:, mains], w_out[:, mains], w_in[:, tails], w_out[:, tails]], axis=1
    )


def mlp_body(place, n_own, n_far, s_own, s_far, *refs):
    blocks, outs, (whole, act, grad) = refs[:16], refs[16:20], refs[20:]
    rows, width = blocks[0].shape
    _, tokens, half = n_own.shape
    core = place[1]
    main, tail = split_of(width)
    for index, block in enumerate(blocks):
        mask = 2 * (index % 8) + index // 8
        source = jnp.bitwise_xor(place[0], mask)
        side = jnp.bitwise_xor(jnp.right_shift(source, 3), place[1])
        start = side * half + jnp.bitwise_and(source, 7) * rows
        whole[pl.ds(pl.multiple_of(start, 8), rows), :] = block[...]
    lower = lax.broadcasted_iota(jnp.int32, (tokens, 128), 1) < tail

    def product(pair, parts):
        def side(left, start):
            weights = jnp.concatenate(
                [whole[start : start + half, at : at + size] for at, size in parts], axis=1
            )
            return jnp.dot(left, weights, preferred_element_type=jnp.float32)

        return side(pair[core], 0) + side(pair[1 - core], half)

    last = (2 * main, 128)
    pieces = spans(main, 256)
    for group, (n_pair, s_pair) in enumerate(((n_own, s_own), (n_far, s_far))):
        where = slice(group * tokens, (group + 1) * tokens)
        for at, size in pieces:
            final = at + size == main
            hidden = product(n_pair, [(at, size)] + ([last] if final else []))
            slopes = product(s_pair, [(main + at, size)] + ([last] if final else []))
            if final:
                moved = pltpu.roll(slopes[:, size:], tail, 1)
                slopes = jnp.concatenate([slopes[:, :size], moved], axis=1)
            cumulative = 0.5 * (1.0 + lax.erf(hidden * (1.0 / math.sqrt(2.0))))
            slope = cumulative + hidden * jnp.exp(-0.5 * hidden * hidden) * (
                1.0 / math.sqrt(2.0 * math.pi)
            )
            value = hidden * cumulative
            back = slopes * slope
            if final:
                upper = pltpu.roll(jnp.where(lower, value[:, size:], 0.0), tail, 1)
                value = jnp.concatenate([value[:, :size], upper], axis=1)
                back = jnp.concatenate(
                    [back[:, :size], jnp.where(lower, back[:, size:], 0.0)], axis=1
                )
            act[where, at : at + value.shape[1]] = value.astype(jnp.bfloat16)
            grad[where, at : at + value.shape[1]] = back.astype(jnp.bfloat16)
    back_products(grad, whole, 0, outs)


def back_products(left, whole, first, outs):
    half = whole.shape[0] // 2
    tokens = left.shape[0] // 2
    main, _ = split_of(whole.shape[1])
    number = 0
    for side in (1, 0):
        for group in (1, 0):
            out = outs[number]
            number += 1
            for at, size in spans(half, 256):
                chosen = slice(side * half + at, side * half + at + size)
                weights = jnp.concatenate(
                    [whole[chosen, first : first + main], whole[chosen, 2 * main :]], axis=1
                )
                out[:, at : at + size] = lax.dot_general(
                    left[group * tokens : (group + 1) * tokens, :],
                    weights,
                    (((1,), (1,)), ((), ())),
                    preferred_element_type=jnp.float32,
                )


def branch_body(act, whole, *outs):
    main, _ = split_of(whole.shape[1])
    back_products(act, whole, main, outs)


def mlp(place, normed, scaled, blocks):
    _, tokens, half = normed[0].shape
    rows, width = blocks[0].shape
    main, tail = split_of(width)
    parts = (f32(tokens, half),) * 4
    *grads, whole, act = call(
        mlp_body,
        (*parts, bf16(2 * half, width), bf16(2 * tokens, main + 128)),
        (*normed, *scaled, *blocks),
        "mlp",
        scalars=(place,),
        scratch=[pltpu.VMEM((2 * tokens, main + 128), jnp.bfloat16)],
        flops=6 * tokens * half * 2 * width,
        limit=32,
    )
    acts = call(branch_body, parts, (act, whole), "branch", flops=2 * tokens * half * 2 * width)
    return *grads, *acts


def joined_body(mine, other, out):
    out[...] = (mine[...] + other[...]).astype(jnp.bfloat16)


def joined(mine, other):
    return call(joined_body, (bf16(*mine.shape),), (mine, other), "joined", flops=mine.size)[0]


def grad_body(mine, other, across, normal, params, norm_grad, stats):
    value = mine[...] + other[...] + across[...].astype(jnp.float32)
    norm_grad[...] = value
    hat = value * params[0:1, :]
    stats[:, 0:1] = jnp.sum(hat, axis=1, keepdims=True)
    stats[:, 1:2] = jnp.sum(hat * normal[...], axis=1, keepdims=True)


def field_body(place, norm_grad, mine, other, normal, inverse, params, field, direct, handed):
    rows, breadth, width = field.shape
    first = (mine[:, 0:1] + other[:, 0:1]) * (0.5 / width)
    second = (mine[:, 1:2] + other[:, 1:2]) * (0.5 / width)
    value = inverse[...] * (norm_grad[...] * params[0:1, :] - first - normal[...] * second)
    value = value.reshape(rows, breadth, width)
    field[...] = value
    narrow = value.astype(jnp.bfloat16)
    even = jnp.bitwise_and(place[0], 1) == 0

    @pl.when(even)
    def _():
        direct[...] = narrow[rows - 3 :]
        handed[...] = narrow[:3]

    @pl.when(jnp.logical_not(even))
    def _():
        direct[...] = narrow[:3]
        handed[...] = narrow[rows - 3 :]


def result_body(place, image, mine, other, across, cot, params, *refs):
    branch = mine[...] + other[...] + across[...].astype(jnp.float32)
    result = refs[4]
    result[...] = (image[...].astype(jnp.float32) + params[2:3, :] * branch).astype(jnp.bfloat16)
    last = jnp.sum(cot[...].astype(jnp.float32) * branch, axis=0, keepdims=True)
    mine_is = jnp.bitwise_and(place[0], 3)
    for mask in range(4):
        chunk, out = refs[mask], refs[5 + mask]
        out[...] = chunk[...]

        @pl.when(jnp.bitwise_xor(mine_is, mask) == 1)
        def _():
            out[0, 7:8, :] = last


def terms_body(
    place, field, near, middle, beyond, norm_grad, normal, c0, c1, c2, c3, rows_all, moved, sums
):
    rows, breadth, width = middle.shape
    fill(rows_all, place, near, middle, beyond)
    clear_borders(moved, breadth)
    sums[...] = jnp.zeros_like(sums)

    def part(lanes):
        moved[:, 8 : 8 + breadth, 0 : lanes.size] = field[:, :, lanes]
        for col in range(7):
            total = [None] * 7
            for at in range(rows):
                values = moved[at, 11 - col : 11 - col + breadth, 0 : lanes.size]
                for tap in range(7):
                    term = values * rows_all[at + tap, :, lanes]
                    term = jnp.sum(term.reshape(breadth // 8, 8, term.shape[1]), axis=0)
                    total[tap] = term if total[tap] is None else total[tap] + term
            for tap in range(7):
                sums[tap, col : col + 1, lanes] = jnp.sum(total[tap], axis=0, keepdims=True)

    each_lanes(width, part)
    sums[0, 7:8, :] = jnp.sum(norm_grad[...] * normal[...], axis=0, keepdims=True)
    sums[1, 7:8, :] = jnp.sum(norm_grad[...], axis=0, keepdims=True)
    for mask, chunk in enumerate((c0, c1, c2, c3)):
        chunk[...] = sums[pl.ds(2 * jnp.bitwise_xor(jnp.bitwise_and(place[0], 3), mask), 2)]


def back_body(place, near, middle, beyond, kernel, cot, out, rows_all, shifted):
    rows, breadth, width = middle.shape
    fill(rows_all, place, near, middle, beyond)
    clear_borders(shifted, breadth)

    def part(lanes):
        for row, value in enumerate(filtered(rows_all, kernel, shifted, rows, breadth, lanes, True)):
            out[row, :, lanes] = (cot[row, :, lanes].astype(jnp.float32) + value).astype(
                jnp.bfloat16
            )

    each_lanes(width, part)


def final_body(factor, place, c0, c1, c2, c3, kernel_sum, param_sum, sums):
    for mask, chunk in enumerate((c0, c1, c2, c3)):
        index = 2 * jnp.bitwise_xor(jnp.bitwise_and(place[0], 3), mask)
        sums[pl.ds(index, 2)] = chunk[...] * factor
    kernel_sum[...] = sums[0:7, 0:7, :]
    for row in range(3):
        param_sum[row : row + 1, :] = sums[row, 7:8, :]


def paired(image, kernel, ln_gain, ln_bias, layer_scale, w_in, w_out, cotangent):
    slab_rows, grid_cols, width_part = image.shape
    tokens = slab_rows * grid_cols
    row = lax.axis_index("row").astype(jnp.int32)
    column = lax.axis_index("col").astype(jnp.int32)
    place = jnp.stack([row, column])
    even = (row & 1) == 0
    direct, handed = edges(even, image[:3], image[slab_rows - 3 :])
    next_rows, beyond_rows = neighbours(direct, handed)

    w_in = after(w_in, direct, handed)
    first, second = packed(w_in, w_out.T, 0), packed(w_in, w_out.T, 1)
    near = {0: jnp.where(even, first, second)}
    far = {0: exchanged(jnp.where(even, second, first), 1)}
    near[8] = exchanged(near[0], 8)
    near[2] = exchanged(near[0], 2)
    near[4] = exchanged(after(near[0], near[2]), 4)
    shape = pltpu.VMEM((slab_rows + 6, grid_cols, width_part), jnp.float32)
    wide = pltpu.VMEM((7, slab_rows, grid_cols + 16, 128), jnp.float32)
    macs = 98 * tokens * width_part
    conved, stats = call(
        conv_body,
        (f32(tokens, width_part), f32(tokens, 2)),
        (next_rows, image, after(beyond_rows, far[0], near[2]), kernel),
        "conv",
        scalars=(place,),
        scratch=[shape, wide],
        flops=macs * 1000,
    )
    far[2] = exchanged(after(far[0], near[2]), 2)
    far[8] = exchanged(after(far[0], near[8]), 8)
    near[10] = exchanged(after(near[8], next_rows), 2)
    near[6] = exchanged(after(near[4], far[2]), 2)
    near[12] = exchanged(after(near[8], near[4]), 4)
    far[10] = exchanged(after(far[8], near[6]), 2)
    far[12] = exchanged(far[8], 4)
    near[14] = exchanged(after(near[12], near[10]), 2)
    far[4] = exchanged(after(far[0], near[12]), 4)
    far[14] = exchanged(after(far[12], far[10]), 2)
    far[6] = exchanged(after(far[2], far[12]), 4)
    weights = [near[m] for m in range(0, 16, 2)] + [far[m] for m in range(0, 16, 2)]

    params = jnp.stack([ln_gain, ln_bias, layer_scale]).reshape(3, 2, width_part)
    params = lax.dynamic_index_in_dim(params, column, 1, False)
    flat_cot = cotangent.reshape(tokens, width_part)
    scaled = (flat_cot.astype(jnp.float32) * params[2]).astype(jnp.bfloat16)
    scaled_far = exchanged(after(scaled, next_rows), 1)
    scaled_all = (both(scaled), both(scaled_far))

    normal, inverse, normed = call(
        norm_body,
        (f32(tokens, width_part), f32(tokens, 1), bf16(tokens, width_part)),
        (conved, stats, siblings(stats), params),
        "norm",
        flops=6 * tokens * width_part,
    )
    normed_far = exchanged(after(normed, scaled_far), 1)
    normed_all = (both(normed), both(normed_far))

    outs = mlp(place, normed_all, scaled_all, weights)
    grad_there_far, grad_there, grad_far, grad_own = outs[:4]
    act_there_far, act_there, act_far, act_own = outs[4:]
    grad_across = exchanged(joined(grad_far, siblings(grad_there_far)), 1)
    act_across = exchanged(after(joined(act_far, siblings(act_there_far)), grad_across), 1)

    norm_grad, back_stats = call(
        grad_body,
        (f32(tokens, width_part), f32(tokens, 2)),
        (grad_own, siblings(grad_there), grad_across, normal, params),
        "grad",
        flops=6 * tokens * width_part,
    )
    field, direct, handed = call(
        field_body,
        (
            f32(slab_rows, grid_cols, width_part),
            bf16(3, grid_cols, width_part),
            bf16(3, grid_cols, width_part),
        ),
        (norm_grad, back_stats, siblings(back_stats), normal, inverse, params),
        "field",
        scalars=(place,),
        flops=6 * tokens * width_part,
    )
    field_next, field_beyond = neighbours(direct, handed)
    chunks = call(
        terms_body,
        (f32(2, 8, width_part),) * 4,
        (field, next_rows, image, beyond_rows, norm_grad, normal),
        "terms",
        scalars=(place,),
        scratch=[
            shape,
            pltpu.VMEM((slab_rows, grid_cols + 16, 128), jnp.float32),
            pltpu.VMEM((8, 8, width_part), jnp.float32),
        ],
        flops=macs,
    )
    result, *chunks = call(
        result_body,
        (bf16(tokens, width_part), *(f32(2, 8, width_part),) * 4),
        (
            image.reshape(tokens, width_part),
            act_own,
            siblings(act_there),
            act_across,
            flat_cot,
            params,
            *chunks,
        ),
        "result",
        scalars=(place,),
        flops=4 * tokens * width_part,
    )
    total = chunks[0] + exchanged(chunks[1], 1) + exchanged(chunks[2], 2) + exchanged(chunks[3], 3)
    total = total + exchanged(total, 12) + exchanged(total, 8) + exchanged(total, 4)
    totals = (total, exchanged(total, 3), exchanged(total, 2), exchanged(total, 1))
    totals = (totals[0], totals[3], totals[2], totals[1])
    grad_image = call(
        back_body,
        (bf16(slab_rows, grid_cols, width_part),),
        (field_next, after(field, total), field_beyond, kernel, cotangent),
        "back",
        scalars=(place,),
        scratch=[shape, wide],
        flops=macs,
    )[0]
    factor = 1.0 / math.sqrt(tokens * lax.axis_size("row"))
    kernel_sum, param_sum = call(
        functools.partial(final_body, factor),
        (f32(7, 7, width_part), f32(3, width_part)),
        (after(totals[0], grad_image), *totals[1:]),
        "final",
        scalars=(place,),
        scratch=[pltpu.VMEM((8, 8, width_part), jnp.float32)],
    )
    return result.reshape(slab_rows, grid_cols, width_part), grad_image, kernel_sum, param_sum


def padded_2(block, sides, width):
    for axis, dim in sides:
        count = lax.axis_size(axis)
        forward = [(i, i + 1) for i in range(count - 1)]
        backward = [(target, source) for source, target in forward]
        low = lax.ppermute(
            lax.slice_in_dim(block, block.shape[dim] - width, None, axis=dim), axis, forward
        )
        high = lax.ppermute(lax.slice_in_dim(block, 0, width, axis=dim), axis, backward)
        block = jnp.concatenate([low, block, high], axis=dim)
    return block


def depthwise(padded, kernel, height, breadth):
    output = jnp.zeros((height, breadth, kernel.shape[2]), jnp.float32)
    for row_tap in range(7):
        for col_tap in range(7):
            output = (
                output
                + kernel[row_tap, col_tap]
                * padded[row_tap : row_tap + height, col_tap : col_tap + breadth]
            )
    return output


def transposed(padded, kernel, height, breadth):
    output = jnp.zeros((height, breadth, kernel.shape[2]), jnp.float32)
    for row_tap in range(7):
        for col_tap in range(7):
            output = (
                output
                + kernel[row_tap, col_tap]
                * padded[6 - row_tap : 6 - row_tap + height, 6 - col_tap : 6 - col_tap + breadth]
            )
    return output


def gelu_slope(values):
    cumulative = 0.5 * (1.0 + lax.erf(values * (1.0 / math.sqrt(2.0))))
    return cumulative + values * jnp.exp(-0.5 * values * values) * (1.0 / math.sqrt(2.0 * math.pi))


def general(image, kernel, ln_gain, ln_bias, layer_scale, w_in, w_out, cotangent):
    slab_rows, grid_cols, width_part = image.shape
    tokens = slab_rows * grid_cols
    channels = ln_gain.shape[0]
    column = lax.axis_index("col")
    gain_part = lax.dynamic_slice_in_dim(ln_gain, column * width_part, width_part)
    bias_part = lax.dynamic_slice_in_dim(ln_bias, column * width_part, width_part)
    scale_part = lax.dynamic_slice_in_dim(layer_scale, column * width_part, width_part)
    extended = padded_2(image, (("row", 0),), 3)
    padded = jnp.pad(extended.astype(jnp.float32), ((0, 0), (3, 3), (0, 0)))
    conved = depthwise(padded, kernel, slab_rows, grid_cols).reshape(tokens, width_part)
    totals, squares = lax.psum((jnp.sum(conved, axis=1), jnp.sum(conved * conved, axis=1)), "col")
    average = totals / channels
    variance = squares / channels - average * average
    inv_std = lax.rsqrt(variance + epsilon)[:, None]
    normal_part = (conved - average[:, None]) * inv_std
    normed = lax.all_gather(
        (normal_part * gain_part + bias_part).astype(jnp.bfloat16), "col", axis=1, tiled=True
    )
    cot_float = cotangent.reshape(tokens, width_part).astype(jnp.float32)
    scaled = lax.all_gather(
        (cot_float * scale_part).astype(jnp.bfloat16), "col", axis=1, tiled=True
    )
    w_in_all = lax.all_gather(w_in, "row", axis=0, tiled=True)
    w_out_all = lax.all_gather(w_out, "row", axis=1, tiled=True)
    hidden = jnp.dot(normed, w_in_all, preferred_element_type=jnp.float32)
    activated = jax.nn.gelu(hidden, approximate=False).astype(jnp.bfloat16)
    branch_terms = jnp.dot(activated, w_out_all, preferred_element_type=jnp.float32)
    act_grad = jnp.einsum("tc,fc->tf", scaled, w_out_all, preferred_element_type=jnp.float32)
    branch = lax.psum_scatter(branch_terms, "col", scatter_dimension=1, tiled=True)
    result = (image.reshape(tokens, width_part).astype(jnp.float32) + scale_part * branch).astype(
        jnp.bfloat16
    )
    hid_grad = (act_grad * gelu_slope(hidden)).astype(jnp.bfloat16)
    norm_terms = jnp.einsum("tf,cf->tc", hid_grad, w_in_all, preferred_element_type=jnp.float32)
    norm_grad = lax.psum_scatter(norm_terms, "col", scatter_dimension=1, tiled=True)
    grad_hat = norm_grad * gain_part
    first_sum, second_sum = lax.psum(
        (jnp.sum(grad_hat, axis=1), jnp.sum(grad_hat * normal_part, axis=1)), "col"
    )
    conv_grad = inv_std * (
        grad_hat - first_sum[:, None] / channels - normal_part * (second_sum[:, None] / channels)
    )
    grad_field = conv_grad.reshape(slab_rows, grid_cols, width_part)
    grad_extended = padded_2(grad_field, (("row", 0),), 3)
    grad_padded = jnp.pad(grad_extended, ((0, 0), (3, 3), (0, 0)))
    grad_image = (
        cot_float.reshape(slab_rows, grid_cols, width_part)
        + transposed(grad_padded, kernel, slab_rows, grid_cols)
    ).astype(jnp.bfloat16)
    kernel_terms = jnp.stack(
        [
            jnp.stack(
                [
                    jnp.sum(
                        grad_field
                        * padded[row_tap : row_tap + slab_rows, col_tap : col_tap + grid_cols],
                        axis=(0, 1),
                    )
                    for col_tap in range(7)
                ]
            )
            for row_tap in range(7)
        ]
    )
    param_terms = jnp.stack(
        [
            jnp.sum(norm_grad * normal_part, axis=0),
            jnp.sum(norm_grad, axis=0),
            jnp.sum(cot_float * branch, axis=0),
        ]
    )
    kernel_sum, param_sum = lax.psum((kernel_terms, param_terms), "row")
    factor = 1.0 / math.sqrt(tokens * lax.axis_size("row"))
    return (
        result.reshape(slab_rows, grid_cols, width_part),
        grad_image,
        kernel_sum * factor,
        param_sum * factor,
    )


def local(*arguments):
    if lax.axis_size("row") == 16:
        return paired(*arguments)
    return general(*arguments)


def solution(mesh):
    in_specs = (
        P(("groups", "row"), None, "col"),
        P(None, None, "col"),
        P(),
        P(),
        P(),
        P("row", "col"),
        P("col", "row"),
        P(("groups", "row"), None, "col"),
    )
    out_specs = (
        P(("groups", "row"), None, "col"),
        P(("groups", "row"), None, "col"),
        P("groups", None, "col"),
        P("groups", "col"),
    )
    return jax.shard_map(local, mesh=mesh, in_specs=in_specs, out_specs=out_specs, check_vma=False)
```

```python
import functools
import math

import jax
import jax.numpy as jnp
from jax import lax
from jax.experimental import pallas as pl
from jax.experimental.pallas import tpu as pltpu
from jax.sharding import PartitionSpec as P

epsilon = 1e-06
VMEM = pl.BlockSpec(memory_space=pltpu.VMEM)
SMEM = pl.BlockSpec(memory_space=pltpu.SMEM)


def sent(value, axis, pairs):
    if value.ndim == 2 and value.shape[1] == 704:
        return lax.ppermute(value.reshape(4, -1, 704), axis, pairs).reshape(value.shape)
    return lax.ppermute(value, axis, pairs)


def exchanged(value, mask):
    count = lax.axis_size("row")
    return sent(value, "row", [(i, i ^ mask) for i in range(count)])


def siblings(value):
    return sent(value, "col", [(0, 1), (1, 0)])


def both(value):
    rows, width = value.shape
    pair = lax.all_gather(value.reshape(4, rows // 4, width), "col", axis=0, tiled=False)
    return pair.reshape(2, rows, width)


def after(value, *others):
    return lax.optimization_barrier((value, *others))[0]


def edges(even, low_rows, high_rows):
    return jnp.where(even, high_rows, low_rows), jnp.where(even, low_rows, high_rows)


def neighbours(direct, handed):
    count = lax.axis_size("row")
    through = exchanged(handed, 1)
    pairs = [(i, i + 2) for i in range(0, count - 2, 2)] + [(i, i - 2) for i in range(3, count, 2)]
    return exchanged(direct, 1), lax.ppermute(through, "row", pairs)


def call(body, outs, operands, name, scalars=(), scratch=(), flops=0, limit=24):
    moved = sum(math.prod(o.shape) * o.dtype.itemsize for o in list(outs) + list(operands))
    return pl.pallas_call(
        body,
        out_shape=tuple(outs),
        in_specs=[SMEM] * len(scalars) + [VMEM] * len(operands),
        out_specs=(VMEM,) * len(outs),
        scratch_shapes=list(scratch),
        compiler_params=pltpu.CompilerParams(vmem_limit_bytes=limit << 20),
        cost_estimate=pl.CostEstimate(flops=flops, bytes_accessed=moved, transcendentals=0),
        name=name,
    )(*scalars, *operands)


def spans(extent, step):
    return [(at, min(step, extent - at)) for at in range(0, extent, step)]


def f32(*shape):
    return jax.ShapeDtypeStruct(shape, jnp.float32)


def bf16(*shape):
    return jax.ShapeDtypeStruct(shape, jnp.bfloat16)


def each_lanes(width, body):
    full = width // 128

    def step(index, carry):
        body(pl.ds(pl.multiple_of(index * 128, 128), 128))
        return carry

    lax.fori_loop(0, full, step, 0)
    if width % 128:
        body(pl.ds(full * 128, width % 128))


def fill(rows_all, place, near, middle, beyond):
    rows = middle.shape[0]
    even = jnp.bitwise_and(place[0], 1) == 0
    rows_all[3 : 3 + rows] = middle[...].astype(jnp.float32)

    @pl.when(even)
    def _():
        rows_all[0:3] = beyond[...].astype(jnp.float32)
        rows_all[3 + rows :] = near[...].astype(jnp.float32)

    @pl.when(jnp.logical_not(even))
    def _():
        rows_all[0:3] = near[...].astype(jnp.float32)
        rows_all[3 + rows :] = beyond[...].astype(jnp.float32)


def clear_borders(ref, breadth):
    edge = ref.shape[:-2] + (8, ref.shape[-1])
    ref[..., 0:8, :] = jnp.zeros(edge, jnp.float32)
    ref[..., 8 + breadth :, :] = jnp.zeros(edge, jnp.float32)


def filtered(rows_all, kernel, shifted, rows, breadth, lanes, flip):
    size = lanes.size
    for col in range(7):
        total = [None] * rows
        for row in range(rows + 6):
            block = rows_all[row, :, lanes]
            for tap in range(7):
                at = row - tap
                if 0 <= at < rows:
                    a, b = (6 - tap, 6 - col) if flip else (tap, col)
                    term = kernel[a, b : b + 1, lanes] * block
                    total[at] = term if total[at] is None else total[at] + term
        for at in range(rows):
            shifted[col, at, 8 : 8 + breadth, 0:size] = total[at]
    results = []
    for at in range(rows):
        value = shifted[0, at, 5 : 5 + breadth, 0:size]
        for col in range(1, 7):
            value = value + shifted[col, at, 5 + col : 5 + col + breadth, 0:size]
        results.append(value)
    return results


def conv_body(place, near, middle, beyond, kernel, conved, stats, rows_all, shifted):
    rows, breadth, width = middle.shape
    fill(rows_all, place, near, middle, beyond)
    clear_borders(shifted, breadth)

    def part(lanes):
        for row, value in enumerate(filtered(rows_all, kernel, shifted, rows, breadth, lanes, False)):
            conved[row * breadth : (row + 1) * breadth, lanes] = value

    each_lanes(width, part)
    values = conved[...]
    mean = jnp.sum(values, axis=1, keepdims=True) * (1.0 / width)
    centred = values - mean
    stats[:, 0:1] = mean
    stats[:, 1:2] = jnp.sum(centred * centred, axis=1, keepdims=True)


def norm_body(conved, mine, other, params, normal, inverse, normed):
    width = conved.shape[1]
    average = 0.5 * (mine[:, 0:1] + other[:, 0:1])
    apart = mine[:, 0:1] - other[:, 0:1]
    variance = (mine[:, 1:2] + other[:, 1:2]) * (0.5 / width) + 0.25 * apart * apart
    inv_std = lax.rsqrt(variance + epsilon)
    value = (conved[...] - average) * inv_std
    normal[...] = value
    inverse[...] = inv_std
    normed[...] = (value * params[0:1, :] + params[1:2, :]).astype(jnp.bfloat16)


def split_of(width):
    main = width // 2 // 128 * 128
    return main, width // 2 - main


def packed(w_in, w_out, which):
    main, tail = split_of(w_in.shape[1])
    mains = slice(which * main, (which + 1) * main)
    tails = slice(2 * main + which * tail, 2 * main + (which + 1) * tail)
    return jnp.concatenate(
        [w_in[:, mains], w_out[:, mains], w_in[:, tails], w_out[:, tails]], axis=1
    )


def mlp_body(place, n_own, n_far, s_own, s_far, *refs):
    blocks, outs, (whole, act, grad) = refs[:16], refs[16:20], refs[20:]
    rows, width = blocks[0].shape
    _, tokens, half = n_own.shape
    core = place[1]
    main, tail = split_of(width)
    for index, block in enumerate(blocks):
        mask = (0, 1, 4, 5, 8, 9, 12, 13)[index % 8] + 2 * (index // 8)
        source = jnp.bitwise_xor(place[0], mask)
        side = jnp.bitwise_xor(jnp.right_shift(source, 3), place[1])
        start = side * half + jnp.bitwise_and(source, 7) * rows
        whole[pl.ds(pl.multiple_of(start, 8), rows), :] = block[...]
    lower = lax.broadcasted_iota(jnp.int32, (tokens, 128), 1) < tail

    def product(pair, parts):
        def side(left, start):
            weights = jnp.concatenate(
                [whole[start : start + half, at : at + size] for at, size in parts], axis=1
            )
            return jnp.dot(left, weights, preferred_element_type=jnp.float32)

        return side(pair[core], 0) + side(pair[1 - core], half)

    last = (2 * main, 128)
    pieces = spans(main, 256)
    for group, (n_pair, s_pair) in enumerate(((n_own, s_own), (n_far, s_far))):
        where = slice(group * tokens, (group + 1) * tokens)
        for at, size in pieces:
            final = at + size == main
            hidden = product(n_pair, [(at, size)] + ([last] if final else []))
            slopes = product(s_pair, [(main + at, size)] + ([last] if final else []))
            if final:
                moved = pltpu.roll(slopes[:, size:], tail, 1)
                slopes = jnp.concatenate([slopes[:, :size], moved], axis=1)
            cumulative = 0.5 * (1.0 + lax.erf(hidden * (1.0 / math.sqrt(2.0))))
            slope = cumulative + hidden * jnp.exp(-0.5 * hidden * hidden) * (
                1.0 / math.sqrt(2.0 * math.pi)
            )
            value = hidden * cumulative
            back = slopes * slope
            if final:
                upper = pltpu.roll(jnp.where(lower, value[:, size:], 0.0), tail, 1)
                value = jnp.concatenate([value[:, :size], upper], axis=1)
                back = jnp.concatenate(
                    [back[:, :size], jnp.where(lower, back[:, size:], 0.0)], axis=1
                )
            act[where, at : at + value.shape[1]] = value.astype(jnp.bfloat16)
            grad[where, at : at + value.shape[1]] = back.astype(jnp.bfloat16)
    back_products(grad, whole, 0, outs)


def back_products(left, whole, first, outs):
    half = whole.shape[0] // 2
    tokens = left.shape[0] // 2
    main, _ = split_of(whole.shape[1])
    number = 0
    for side in (1, 0):
        for group in (1, 0):
            out = outs[number]
            number += 1
            for at, size in spans(half, 256):
                chosen = slice(side * half + at, side * half + at + size)
                weights = jnp.concatenate(
                    [whole[chosen, first : first + main], whole[chosen, 2 * main :]], axis=1
                )
                out[:, at : at + size] = lax.dot_general(
                    left[group * tokens : (group + 1) * tokens, :],
                    weights,
                    (((1,), (1,)), ((), ())),
                    preferred_element_type=jnp.float32,
                )


def branch_body(act, whole, *outs):
    main, _ = split_of(whole.shape[1])
    back_products(act, whole, main, outs)


def mlp(place, normed, scaled, blocks):
    _, tokens, half = normed[0].shape
    rows, width = blocks[0].shape
    main, tail = split_of(width)
    parts = (f32(tokens, half),) * 4
    *grads, whole, act = call(
        mlp_body,
        (*parts, bf16(2 * half, width), bf16(2 * tokens, main + 128)),
        (*normed, *scaled, *blocks),
        "mlp",
        scalars=(place,),
        scratch=[pltpu.VMEM((2 * tokens, main + 128), jnp.bfloat16)],
        flops=6 * tokens * half * 2 * width,
        limit=32,
    )
    acts = call(branch_body, parts, (act, whole), "branch", flops=2 * tokens * half * 2 * width)
    return *grads, *acts


def joined_body(mine, other, out):
    out[...] = (mine[...] + other[...]).astype(jnp.bfloat16)


def joined(mine, other):
    return call(joined_body, (bf16(*mine.shape),), (mine, other), "joined", flops=mine.size)[0]


def grad_body(mine, other, across, normal, params, norm_grad, stats):
    value = mine[...] + other[...] + across[...].astype(jnp.float32)
    norm_grad[...] = value
    hat = value * params[0:1, :]
    stats[:, 0:1] = jnp.sum(hat, axis=1, keepdims=True)
    stats[:, 1:2] = jnp.sum(hat * normal[...], axis=1, keepdims=True)


def field_body(place, norm_grad, mine, other, normal, inverse, params, field, direct, handed):
    rows, breadth, width = field.shape
    first = (mine[:, 0:1] + other[:, 0:1]) * (0.5 / width)
    second = (mine[:, 1:2] + other[:, 1:2]) * (0.5 / width)
    value = inverse[...] * (norm_grad[...] * params[0:1, :] - first - normal[...] * second)
    value = value.reshape(rows, breadth, width)
    field[...] = value
    narrow = value.astype(jnp.bfloat16)
    even = jnp.bitwise_and(place[0], 1) == 0

    @pl.when(even)
    def _():
        direct[...] = narrow[rows - 3 :]
        handed[...] = narrow[:3]

    @pl.when(jnp.logical_not(even))
    def _():
        direct[...] = narrow[:3]
        handed[...] = narrow[rows - 3 :]


def result_body(image, mine, other, across, cot, params, c0, c1, c2, c3, result, total):
    branch = mine[...] + other[...] + across[...].astype(jnp.float32)
    result[...] = (image[...].astype(jnp.float32) + params[2:3, :] * branch).astype(jnp.bfloat16)
    total[...] = c0[...] + c1[...] + c2[...] + c3[...]
    total[0, 7:8, :] = jnp.sum(cot[...].astype(jnp.float32) * branch, axis=0, keepdims=True)


def terms_body(
    place, field, near, middle, beyond, norm_grad, normal, c0, c1, c2, c3, rows_all, moved, sums
):
    rows, breadth, width = middle.shape
    fill(rows_all, place, near, middle, beyond)
    clear_borders(moved, breadth)
    sums[...] = jnp.zeros_like(sums)

    def part(lanes):
        moved[:, 8 : 8 + breadth, 0 : lanes.size] = field[:, :, lanes]
        for col in range(7):
            total = [None] * 7
            for at in range(rows):
                values = moved[at, 11 - col : 11 - col + breadth, 0 : lanes.size]
                for tap in range(7):
                    term = values * rows_all[at + tap, :, lanes]
                    term = jnp.sum(term.reshape(breadth // 8, 8, term.shape[1]), axis=0)
                    total[tap] = term if total[tap] is None else total[tap] + term
            for tap in range(7):
                sums[tap, col : col + 1, lanes] = jnp.sum(total[tap], axis=0, keepdims=True)

    each_lanes(width, part)
    sums[7, 0:1, :] = jnp.sum(norm_grad[...] * normal[...], axis=0, keepdims=True)
    sums[7, 1:2, :] = jnp.sum(norm_grad[...], axis=0, keepdims=True)
    for mask, chunk in enumerate((c0, c1, c2, c3)):
        chunk[...] = sums[pl.ds(2 * jnp.bitwise_xor(jnp.bitwise_and(place[0], 3), mask), 2)]


def back_body(place, near, middle, beyond, kernel, cot, out, rows_all, shifted):
    rows, breadth, width = middle.shape
    fill(rows_all, place, near, middle, beyond)
    clear_borders(shifted, breadth)

    def part(lanes):
        for row, value in enumerate(filtered(rows_all, kernel, shifted, rows, breadth, lanes, True)):
            out[row, :, lanes] = (cot[row, :, lanes].astype(jnp.float32) + value).astype(
                jnp.bfloat16
            )

    each_lanes(width, part)


def final_body(factor, place, c0, c1, c2, c3, kernel_sum, param_sum, sums):
    for mask, chunk in enumerate((c0, c1, c2, c3)):
        index = 2 * jnp.bitwise_xor(jnp.bitwise_and(place[0], 3), mask)
        sums[pl.ds(index, 2)] = chunk[...] * factor
    kernel_sum[...] = sums[0:7, 0:7, :]
    param_sum[0:2, :] = sums[7, 0:2, :]
    param_sum[2:3, :] = sums[0, 7:8, :] + sums[2, 7:8, :] + sums[4, 7:8, :] + sums[6, 7:8, :]


def paired(image, kernel, ln_gain, ln_bias, layer_scale, w_in, w_out, cotangent):
    slab_rows, grid_cols, width_part = image.shape
    tokens = slab_rows * grid_cols
    row = lax.axis_index("row").astype(jnp.int32)
    column = lax.axis_index("col").astype(jnp.int32)
    place = jnp.stack([row, column])
    even = (row & 1) == 0
    direct, handed = edges(even, image[:3], image[slab_rows - 3 :])
    next_rows, beyond_rows = neighbours(direct, handed)

    w_in = after(w_in, direct, handed)
    first, second = packed(w_in, w_out.T, 0), packed(w_in, w_out.T, 1)
    upper = (row & 2) == 0
    near = {0: jnp.where(upper, first, second)}
    far = {0: exchanged(jnp.where(upper, second, first), 2)}
    near[8] = exchanged(near[0], 8)
    near[1] = exchanged(near[0], 1)
    near[4] = exchanged(after(near[0], near[1]), 4)
    shape = pltpu.VMEM((slab_rows + 6, grid_cols, width_part), jnp.float32)
    wide = pltpu.VMEM((7, slab_rows, grid_cols + 16, 128), jnp.float32)
    macs = 98 * tokens * width_part
    conved, stats = call(
        conv_body,
        (f32(tokens, width_part), f32(tokens, 2)),
        (next_rows, image, beyond_rows, kernel),
        "conv",
        scalars=(place,),
        scratch=[shape, wide],
        flops=macs * 1000,
    )
    far[1] = exchanged(after(far[0], near[1]), 1)
    far[8] = exchanged(after(far[0], near[8]), 8)
    near[9] = exchanged(after(near[8], next_rows), 1)
    near[5] = exchanged(after(near[4], far[1]), 1)
    near[12] = exchanged(after(near[8], near[4]), 4)
    far[9] = exchanged(after(far[8], near[5]), 1)
    far[12] = exchanged(far[8], 4)
    near[13] = exchanged(after(near[12], near[9]), 1)
    far[4] = exchanged(after(far[0], near[12]), 4)
    far[13] = exchanged(after(far[12], far[9]), 1)
    far[5] = exchanged(after(far[1], far[12]), 4)
    masks = (0, 1, 4, 5, 8, 9, 12, 13)
    weights = [near[m] for m in masks] + [far[m] for m in masks]

    params = jnp.stack([ln_gain, ln_bias, layer_scale]).reshape(3, 2, width_part)
    params = lax.dynamic_index_in_dim(params, column, 1, False)
    flat_cot = cotangent.reshape(tokens, width_part)
    scaled = (flat_cot.astype(jnp.float32) * params[2]).astype(jnp.bfloat16)
    scaled_far = exchanged(after(scaled, next_rows), 2)
    scaled_all = (both(scaled), both(scaled_far))

    normal, inverse, normed = call(
        norm_body,
        (f32(tokens, width_part), f32(tokens, 1), bf16(tokens, width_part)),
        (conved, stats, siblings(stats), params),
        "norm",
        flops=6 * tokens * width_part,
    )
    normed_far = exchanged(after(normed, scaled_far), 2)
    normed_all = (both(normed), both(normed_far))

    outs = mlp(place, normed_all, scaled_all, weights)
    grad_there_far, grad_there, grad_far, grad_own = outs[:4]
    act_there_far, act_there, act_far, act_own = outs[4:]
    grad_across = exchanged(joined(grad_far, siblings(grad_there_far)), 2)
    act_across = exchanged(after(joined(act_far, siblings(act_there_far)), grad_across), 2)

    norm_grad, back_stats = call(
        grad_body,
        (f32(tokens, width_part), f32(tokens, 2)),
        (grad_own, siblings(grad_there), grad_across, normal, params),
        "grad",
        flops=6 * tokens * width_part,
    )
    field, direct, handed = call(
        field_body,
        (
            f32(slab_rows, grid_cols, width_part),
            bf16(3, grid_cols, width_part),
            bf16(3, grid_cols, width_part),
        ),
        (norm_grad, back_stats, siblings(back_stats), normal, inverse, params),
        "field",
        scalars=(place,),
        flops=6 * tokens * width_part,
    )
    field_next, field_beyond = neighbours(direct, handed)
    chunks = call(
        terms_body,
        (f32(2, 8, width_part),) * 4,
        (field, next_rows, image, beyond_rows, norm_grad, normal),
        "terms",
        scalars=(place,),
        scratch=[
            shape,
            pltpu.VMEM((slab_rows, grid_cols + 16, 128), jnp.float32),
            pltpu.VMEM((8, 8, width_part), jnp.float32),
        ],
        flops=macs,
    )
    result, total = call(
        result_body,
        (bf16(tokens, width_part), f32(2, 8, width_part)),
        (
            image.reshape(tokens, width_part),
            act_own,
            siblings(act_there),
            act_across,
            flat_cot,
            params,
            chunks[0],
            exchanged(chunks[1], 1),
            exchanged(chunks[2], 2),
            exchanged(chunks[3], 3),
        ),
        "result",
        flops=4 * tokens * width_part,
    )
    total = total + exchanged(total, 12) + exchanged(total, 8) + exchanged(total, 4)
    totals = (total, exchanged(total, 3), exchanged(total, 2), exchanged(total, 1))
    totals = (totals[0], totals[3], totals[2], totals[1])
    grad_image = call(
        back_body,
        (bf16(slab_rows, grid_cols, width_part),),
        (field_next, after(field, total), field_beyond, kernel, cotangent),
        "back",
        scalars=(place,),
        scratch=[shape, wide],
        flops=macs,
    )[0]
    factor = 1.0 / math.sqrt(tokens * lax.axis_size("row"))
    kernel_sum, param_sum = call(
        functools.partial(final_body, factor),
        (f32(7, 7, width_part), f32(3, width_part)),
        (after(totals[0], grad_image), *totals[1:]),
        "final",
        scalars=(place,),
        scratch=[pltpu.VMEM((8, 8, width_part), jnp.float32)],
    )
    return result.reshape(slab_rows, grid_cols, width_part), grad_image, kernel_sum, param_sum


def padded_2(block, sides, width):
    for axis, dim in sides:
        count = lax.axis_size(axis)
        forward = [(i, i + 1) for i in range(count - 1)]
        backward = [(target, source) for source, target in forward]
        low = lax.ppermute(
            lax.slice_in_dim(block, block.shape[dim] - width, None, axis=dim), axis, forward
        )
        high = lax.ppermute(lax.slice_in_dim(block, 0, width, axis=dim), axis, backward)
        block = jnp.concatenate([low, block, high], axis=dim)
    return block


def depthwise(padded, kernel, height, breadth):
    output = jnp.zeros((height, breadth, kernel.shape[2]), jnp.float32)
    for row_tap in range(7):
        for col_tap in range(7):
            output = (
                output
                + kernel[row_tap, col_tap]
                * padded[row_tap : row_tap + height, col_tap : col_tap + breadth]
            )
    return output


def transposed(padded, kernel, height, breadth):
    output = jnp.zeros((height, breadth, kernel.shape[2]), jnp.float32)
    for row_tap in range(7):
        for col_tap in range(7):
            output = (
                output
                + kernel[row_tap, col_tap]
                * padded[6 - row_tap : 6 - row_tap + height, 6 - col_tap : 6 - col_tap + breadth]
            )
    return output


def gelu_slope(values):
    cumulative = 0.5 * (1.0 + lax.erf(values * (1.0 / math.sqrt(2.0))))
    return cumulative + values * jnp.exp(-0.5 * values * values) * (1.0 / math.sqrt(2.0 * math.pi))


def general(image, kernel, ln_gain, ln_bias, layer_scale, w_in, w_out, cotangent):
    slab_rows, grid_cols, width_part = image.shape
    tokens = slab_rows * grid_cols
    channels = ln_gain.shape[0]
    column = lax.axis_index("col")
    gain_part = lax.dynamic_slice_in_dim(ln_gain, column * width_part, width_part)
    bias_part = lax.dynamic_slice_in_dim(ln_bias, column * width_part, width_part)
    scale_part = lax.dynamic_slice_in_dim(layer_scale, column * width_part, width_part)
    extended = padded_2(image, (("row", 0),), 3)
    padded = jnp.pad(extended.astype(jnp.float32), ((0, 0), (3, 3), (0, 0)))
    conved = depthwise(padded, kernel, slab_rows, grid_cols).reshape(tokens, width_part)
    totals, squares = lax.psum((jnp.sum(conved, axis=1), jnp.sum(conved * conved, axis=1)), "col")
    average = totals / channels
    variance = squares / channels - average * average
    inv_std = lax.rsqrt(variance + epsilon)[:, None]
    normal_part = (conved - average[:, None]) * inv_std
    normed = lax.all_gather(
        (normal_part * gain_part + bias_part).astype(jnp.bfloat16), "col", axis=1, tiled=True
    )
    cot_float = cotangent.reshape(tokens, width_part).astype(jnp.float32)
    scaled = lax.all_gather(
        (cot_float * scale_part).astype(jnp.bfloat16), "col", axis=1, tiled=True
    )
    w_in_all = lax.all_gather(w_in, "row", axis=0, tiled=True)
    w_out_all = lax.all_gather(w_out, "row", axis=1, tiled=True)
    hidden = jnp.dot(normed, w_in_all, preferred_element_type=jnp.float32)
    activated = jax.nn.gelu(hidden, approximate=False).astype(jnp.bfloat16)
    branch_terms = jnp.dot(activated, w_out_all, preferred_element_type=jnp.float32)
    act_grad = jnp.einsum("tc,fc->tf", scaled, w_out_all, preferred_element_type=jnp.float32)
    branch = lax.psum_scatter(branch_terms, "col", scatter_dimension=1, tiled=True)
    result = (image.reshape(tokens, width_part).astype(jnp.float32) + scale_part * branch).astype(
        jnp.bfloat16
    )
    hid_grad = (act_grad * gelu_slope(hidden)).astype(jnp.bfloat16)
    norm_terms = jnp.einsum("tf,cf->tc", hid_grad, w_in_all, preferred_element_type=jnp.float32)
    norm_grad = lax.psum_scatter(norm_terms, "col", scatter_dimension=1, tiled=True)
    grad_hat = norm_grad * gain_part
    first_sum, second_sum = lax.psum(
        (jnp.sum(grad_hat, axis=1), jnp.sum(grad_hat * normal_part, axis=1)), "col"
    )
    conv_grad = inv_std * (
        grad_hat - first_sum[:, None] / channels - normal_part * (second_sum[:, None] / channels)
    )
    grad_field = conv_grad.reshape(slab_rows, grid_cols, width_part)
    grad_extended = padded_2(grad_field, (("row", 0),), 3)
    grad_padded = jnp.pad(grad_extended, ((0, 0), (3, 3), (0, 0)))
    grad_image = (
        cot_float.reshape(slab_rows, grid_cols, width_part)
        + transposed(grad_padded, kernel, slab_rows, grid_cols)
    ).astype(jnp.bfloat16)
    kernel_terms = jnp.stack(
        [
            jnp.stack(
                [
                    jnp.sum(
                        grad_field
                        * padded[row_tap : row_tap + slab_rows, col_tap : col_tap + grid_cols],
                        axis=(0, 1),
                    )
                    for col_tap in range(7)
                ]
            )
            for row_tap in range(7)
        ]
    )
    param_terms = jnp.stack(
        [
            jnp.sum(norm_grad * normal_part, axis=0),
            jnp.sum(norm_grad, axis=0),
            jnp.sum(cot_float * branch, axis=0),
        ]
    )
    kernel_sum, param_sum = lax.psum((kernel_terms, param_terms), "row")
    factor = 1.0 / math.sqrt(tokens * lax.axis_size("row"))
    return (
        result.reshape(slab_rows, grid_cols, width_part),
        grad_image,
        kernel_sum * factor,
        param_sum * factor,
    )


def local(*arguments):
    if lax.axis_size("row") == 16:
        return paired(*arguments)
    return general(*arguments)


def solution(mesh):
    in_specs = (
        P(("groups", "row"), None, "col"),
        P(None, None, "col"),
        P(),
        P(),
        P(),
        P("row", "col"),
        P("col", "row"),
        P(("groups", "row"), None, "col"),
    )
    out_specs = (
        P(("groups", "row"), None, "col"),
        P(("groups", "row"), None, "col"),
        P("groups", None, "col"),
        P("groups", "col"),
    )
    return jax.shard_map(local, mesh=mesh, in_specs=in_specs, out_specs=out_specs, check_vma=False)
```
